512 devices in a mesh: pts: 16 (over z), elem: 32 (over y, x, core).
Axes of the slice: x: 4, y: 4, z: 16, core: 2. Of those that a mesh axis runs over, the one named last changes fastest.
Arguments:
- theta: float32 [1024, 1024], P('elem', 'pts'), may hold values from -3.140625 to 3.140625
- panel_rows: int32 [1024], P('elem'), may hold values from 0 to 1023, each once
- point_rows: int32 [32768], P('pts'), may hold values from 0 to 511
- point_cols: int32 [32768], P('pts'), may hold values from 0 to 255
- direct: float32 [2, 32768], P(None, 'pts'), may hold values from -3 to 3
- noise: float32 [32768], P('pts'), may hold values from 0.05 to 0.5
Outputs:
- phase_grad: float32 [1024, 1024], P('elem', 'pts')
- field: float32 [2, 32768], P(None, 'pts')
The draws below stay inside these ranges and needn't reach their ends.
Inputs may be any that keep to these rules, and one draw needn't show every extreme that they name: `panel_rows`: each lattice row appears once.
All inputs are finite; a program needn't handle non-finite values.
Results may differ from the reference program's by a relative error of at most 0.0004.
Values sent between devices are 32-bit elements; how exact they have to be, the bound alone decides.
No kernel may reach another device: no remote copies, remote signals or barrier semaphores. Data moves between devices by JAX's collectives and lax.ppermute only.
A program may use at most 64 MiB of HBM per device.

```python
import math
import jax
import jax.numpy as jnp
from jax import lax

NX_EL = 1024
NY_EL = 1024
POINTS = 32768


def place_ends(values, stream_key, smallest, largest):
    shape = values.shape
    index_at = [jax.random.randint(jax.random.fold_in(stream_key, axis), (), 0, shape[axis]) for axis in range(len(shape))]
    values = values.at[tuple(index_at)].set(smallest)
    longest = shape.index(max(shape))
    index_at[longest] = (index_at[longest] + 1) % shape[longest]
    return values.at[tuple(index_at)].set(largest)


def level_of(stream_key, shape, cuts, least, top_value):
    loudness = 1.0
    for axis_at, blocks in cuts:
        steps = jax.random.uniform(jax.random.fold_in(jax.random.fold_in(stream_key, 6), axis_at), (blocks,), jnp.float32, least / len(cuts), top_value / len(cuts))
        loudness = loudness * jnp.repeat(jnp.exp(steps), shape[axis_at] // blocks).reshape((-1,) + (1,) * (len(shape) - 1 - axis_at))
    return loudness


def gaussian(key, dims, deviation, bound, cuts=(), held_as=jnp.bfloat16):
    level = level_of(key, dims, cuts, -0.22, 0.18) if cuts else 1.0
    result = jax.random.normal(key, dims, jnp.float32) * deviation * level
    return jnp.minimum(jnp.maximum(result, -bound), bound).astype(held_as)


def setup_inputs(seed: int = 0) -> dict:
    splits = jax.random.split(jax.random.key(seed), 7)
    return {
        "theta": jnp.clip(jax.random.uniform(splits[0], (NX_EL, NY_EL), jnp.float32, -3.140625, 3.140625), -3.140625, 3.140625),
        "panel_rows": jax.random.permutation(splits[1], NX_EL).astype(jnp.int32),
        "point_rows": place_ends(jax.random.randint(splits[2], (POINTS,), 0, 512), jax.random.fold_in(splits[2], 1), 0, 511).astype(jnp.int32),
        "point_cols": place_ends(jax.random.randint(splits[3], (POINTS,), 0, 256), jax.random.fold_in(splits[3], 1), 0, 255).astype(jnp.int32),
        "direct": gaussian(splits[4], (2, POINTS), 0.5, 3.0, ((1, 16),), jnp.float32),
        "noise": jnp.clip(jnp.exp(math.log(0.5) - 2.3025851 * jax.random.uniform(splits[5], (POINTS,), jnp.float32) ** level_of(splits[5], (POINTS,), ((0, 16),), -0.2, 0.2)), 0.05, 0.5),
    }


HIGH = lax.Precision.HIGHEST

def geometry(point_rows, point_cols):
    along_x = (point_rows.astype(jnp.float32) - 255.5) * 0.5
    along_y = (point_cols.astype(jnp.float32) - 127.5) * 0.5
    radius = jnp.sqrt(along_x * along_x + along_y * along_y + 1600.0)
    return (along_x / radius, along_y / radius, 80.0 / (radius * math.sqrt(NX_EL * NY_EL)))

def partial_field(slope_x, slope_y, lattice_x, lattice_y, phase_re, phase_im):
    beam_y = math.pi * slope_y[:, None] * lattice_y[None, :]
    left = jnp.concatenate([jnp.cos(beam_y), jnp.sin(beam_y)], 1)
    right = jnp.concatenate([jnp.concatenate([phase_re.T, phase_im.T], 1), jnp.concatenate([-phase_im.T, phase_re.T], 1)], 0)
    inner = jnp.dot(left, right, precision=HIGH, preferred_element_type=jnp.float32)
    width = phase_re.shape[0]
    inner_re = inner[:, :width]
    inner_im = inner[:, width:]
    beam_x = math.pi * slope_x[:, None] * lattice_x[None, :]
    cos_x = jnp.cos(beam_x)
    sin_x = jnp.sin(beam_x)
    return jnp.stack([lax.optimization_barrier(jnp.sum(cos_x * inner_re - sin_x * inner_im, 1)), lax.optimization_barrier(jnp.sum(cos_x * inner_im + sin_x * inner_re, 1))])

def surface_terms(slope_x, slope_y, q_re, q_im, lattice_x, lattice_y):
    beam_x = math.pi * slope_x[:, None] * lattice_x[None, :]
    cos_x = jnp.cos(beam_x)
    sin_x = jnp.sin(beam_x)
    weight_re = q_re[:, None] * cos_x - q_im[:, None] * sin_x
    weight_im = q_re[:, None] * sin_x + q_im[:, None] * cos_x
    beam_y = math.pi * slope_y[:, None] * lattice_y[None, :]
    left = jnp.concatenate([jnp.cos(beam_y), jnp.sin(beam_y)], 1)
    right = jnp.concatenate([weight_re, weight_im], 1)
    prod = lax.dot_general(left, right, (((0,), (0,)), ((), ())), precision=HIGH, preferred_element_type=jnp.float32)
    rows_y = lattice_y.shape[0]
    cols_x = lattice_x.shape[0]
    sum_re = prod[:rows_y, :cols_x] - prod[rows_y:, cols_x:]
    sum_im = prod[:rows_y, cols_x:] + prod[rows_y:, :cols_x]
    return jnp.concatenate([sum_re, sum_im], 1)

def block_size(points, cols_y):
    return math.gcd(points, min(points, max(256, 524288 // cols_y)))

def field_blocks(slope_x, slope_y, lattice_x, lattice_y, phase_re, phase_im):
    block = block_size(slope_x.shape[0], lattice_y.shape[0])
    count = slope_x.shape[0] // block

    def one_block(pair):
        return partial_field(pair[0], pair[1], lattice_x, lattice_y, phase_re, phase_im)
    parts = lax.map(one_block, (slope_x.reshape(count, block), slope_y.reshape(count, block)))
    return jnp.transpose(parts, (1, 0, 2)).reshape(2, count * block)

def terms_blocks(slope_x, slope_y, q_re, q_im, lattice_x, lattice_y):
    block = block_size(slope_x.shape[0], lattice_y.shape[0])
    count = slope_x.shape[0] // block
    start = jnp.zeros((lattice_y.shape[0], 2 * lattice_x.shape[0]), jnp.float32)

    def step(carry, items):
        return (carry + surface_terms(items[0], items[1], items[2], items[3], lattice_x, lattice_y), None)
    items = (slope_x.reshape(count, block), slope_y.reshape(count, block), q_re.reshape(count, block), q_im.reshape(count, block))
    total, unused = lax.scan(step, start, items)
    return total

def weights(field, scale, noise):
    power = noise + field[0] * field[0] + field[1] * field[1]
    return (field[0] * scale / power, -field[1] * scale / power)

def gradient(terms, phase_re, phase_im):
    cols_x = phase_re.shape[0]
    sum_re = terms[:, :cols_x].T
    sum_im = terms[:, cols_x:].T
    return -2.0 * (phase_re * sum_im + phase_im * sum_re)

def reference(theta, panel_rows, point_rows, point_cols, direct, noise):
    slope_x, slope_y, scale = geometry(point_rows, point_cols)
    phase_re = jnp.cos(theta)
    phase_im = jnp.sin(theta)
    lattice_x = panel_rows.astype(jnp.float32) - (NX_EL - 1) / 2.0
    lattice_y = jnp.arange(NY_EL).astype(jnp.float32) - (NY_EL - 1) / 2.0
    total = field_blocks(slope_x, slope_y, lattice_x, lattice_y, phase_re, phase_im)
    field = direct + scale[None, :] * total
    q_re, q_im = weights(field, scale, noise)
    terms = terms_blocks(slope_x, slope_y, q_re, q_im, lattice_x, lattice_y)
    return (gradient(terms, phase_re, phase_im), field)
```

```python
import math

import jax
import jax.numpy as jnp
from jax import lax
from jax.experimental import pallas as pl
from jax.experimental.pallas import tpu as pltpu
from jax.sharding import PartitionSpec as P

NX_EL = 1024
NY_EL = 1024
CHUNKS = 4
CW = 512
LOW = 128
TWO_PI = 2.0 * math.pi

F32 = jnp.float32
BF16 = jnp.bfloat16


def _fit(func, degree):
    import numpy as np

    nodes = 0.125 + 0.125 * np.cos(np.pi * (np.arange(64) + 0.5) / 64)
    poly = np.polynomial.Chebyshev.fit(nodes, func(np.sqrt(nodes)), degree, domain=[0.0, 0.25])
    return [float(c) for c in poly.convert(kind=np.polynomial.Polynomial).coef]


def _tables():
    import numpy as np

    return (
        _fit(lambda r: np.sin(np.pi * r) / r, 5),
        _fit(lambda r: np.cos(np.pi * r), 5),
    )


SIN_C, COS_C = _tables()


def _horner(x, coefs):
    acc = jnp.full_like(x, coefs[-1])
    for c in coefs[-2::-1]:
        acc = acc * x + c
    return acc


def cos_sin_turns(t):
    r = t - jnp.round(t)
    x = r * r
    s = r * _horner(x, SIN_C)
    c = _horner(x, COS_C)
    two_s = s + s
    return 1.0 - two_s * s, two_s * c


def split(x):
    hi = x.astype(BF16)
    lo = (x - hi.astype(F32)).astype(BF16)
    return hi, lo


def mm(a, b):
    return lax.dot_general(a, b, (((1,), (0,)), ((), ())), preferred_element_type=F32)


def mm_nt(a, b):
    return lax.dot_general(a, b, (((1,), (1,)), ((), ())), preferred_element_type=F32)


def slopes(rows_ref, cols_ref):
    along_x = (rows_ref[...].astype(F32) - 255.5) * 0.5
    along_y = (cols_ref[...].astype(F32) - 127.5) * 0.5
    radius = jnp.sqrt(along_x * along_x + along_y * along_y + 1600.0)
    return along_x / radius, along_y / radius, 80.0 / (radius * 1024.0)


def sides(v):
    out = []
    for h in range(NY_EL // LOW):
        a = v[2 * h]
        b = v[2 * h + 1]
        top = jnp.concatenate([a[:, :64], b[:, :64]], 1)
        low = jnp.concatenate([a[:, 64:], b[:, 64:]], 1)
        out.append(jnp.concatenate([top, low], 0))
    return out


def table_kernel(prow_ref, pcol_ref, rows_ref, low_ref, high_ref, x_ref):
    sx, sy, _ = slopes(prow_ref, pcol_ref)
    sx = sx * 0.5
    sy = sy * 0.5
    low_k = lax.broadcasted_iota(jnp.int32, (LOW, CW), 0).astype(F32) - (LOW - 1) / 2.0
    high_k = (lax.broadcasted_iota(jnp.int32, (8, CW), 0) * LOW).astype(F32) + LOW / 2.0
    lattice_x = rows_ref[...].astype(F32) - (NX_EL - 1) / 2.0
    for r in range(CHUNKS):
        cols = slice(CW * r, CW * r + CW)
        c, s = cos_sin_turns(low_k * sy[r : r + 1])
        hi, lo = split(c)
        low_ref[0:LOW, cols] = hi
        low_ref[2 * LOW : 3 * LOW, cols] = lo
        hi, lo = split(s)
        low_ref[LOW : 2 * LOW, cols] = hi
        low_ref[3 * LOW : 4 * LOW, cols] = lo
        c, s = cos_sin_turns(high_k * sy[r : r + 1])
        high_ref[0:4, cols] = c[0:4]
        high_ref[4:8, cols] = s[0:4]
        c, s = cos_sin_turns(lattice_x * sx[r : r + 1])
        x_ref[0:32, cols] = c
        x_ref[32:64, cols] = s


def field_kernel(theta_ref, low_ref, high_ref, x_ref, part_ref, u_ref):
    c, s = cos_sin_turns(theta_ref[...] * (1.0 / TWO_PI))
    re = sides(c)
    im = sides(s)
    rows = []
    for g in range(4):
        for sign in (1.0, -1.0):
            v_re = re[4 + g] + sign * re[3 - g]
            v_im = im[4 + g] + sign * im[3 - g]
            rows.append(jnp.concatenate([v_re, -v_im], 1))
            rows.append(jnp.concatenate([v_im, v_re], 1))
    for h in range(8):
        u_ref[0:32, 128 * h : 128 * h + 128] = re[h]
        u_ref[32:64, 128 * h : 128 * h + 128] = im[h]
    hi, lo = split(jnp.concatenate(rows, 0))
    both = jnp.concatenate([hi, hi], 1)
    for r in range(CHUNKS):
        cols = slice(CW * r, CW * r + CW)
        p = mm(both, low_ref[:, cols]) + mm(lo, low_ref[0 : 2 * LOW, cols])
        f_re = jnp.zeros((32, CW), F32)
        f_im = jnp.zeros((32, CW), F32)
        for g in range(4):
            hc = high_ref[g : g + 1, cols]
            hs = high_ref[4 + g : 5 + g, cols]
            q = p[128 * g : 128 * g + 128]
            f_re = f_re + (hc * q[0:32] - hs * q[96:128])
            f_im = f_im + (hc * q[32:64] + hs * q[64:96])
        xc = x_ref[0:32, cols]
        xs = x_ref[32:64, cols]
        part_ref[r : r + 1] = jnp.sum(xc * f_re - xs * f_im, 0, keepdims=True)
        part_ref[r + 4 : r + 5] = jnp.sum(xc * f_im + xs * f_re, 0, keepdims=True)


def gradient_kernel(
    parts_ref, direct_ref, noise_ref, prow_ref, pcol_ref, low_ref, high_ref, x_ref, u_ref, field_ref, out_ref, whi_ref, wlo_ref
):
    _, _, scale = slopes(prow_ref, pcol_ref)
    total = jnp.sum(parts_ref[...], 0)
    re = direct_ref[0:4] + scale * total[0:4]
    im = direct_ref[4:8] + scale * total[4:8]
    field_ref[0:4] = re
    field_ref[4:8] = im
    power = noise_ref[...] + re * re + im * im
    q_re = re * scale / power
    q_im = -im * scale / power
    for r in range(CHUNKS):
        cols = slice(CW * r, CW * r + CW)
        a = q_re[r : r + 1]
        b = q_im[r : r + 1]
        xc = x_ref[0:32, cols]
        xs = x_ref[32:64, cols]
        w_re = a * xc - b * xs
        w_im = a * xs + b * xc
        w = jnp.concatenate([w_re, w_im], 0)
        for g in range(4):
            hi, lo = split(w * high_ref[g : g + 1, cols])
            whi_ref[128 * g : 128 * g + 64, cols] = hi
            wlo_ref[128 * g : 128 * g + 64, cols] = lo
            hi, lo = split(w * high_ref[4 + g : 5 + g, cols])
            whi_ref[128 * g + 64 : 128 * g + 128, cols] = hi
            wlo_ref[128 * g + 64 : 128 * g + 128, cols] = lo
    sums = (
        mm_nt(whi_ref[...], low_ref[0 : 2 * LOW])
        + mm_nt(wlo_ref[...], low_ref[0 : 2 * LOW])
        + mm_nt(whi_ref[...], low_ref[2 * LOW :])
    )
    for g in range(4):
        v = sums[128 * g : 128 * g + 128]
        a_re = v[0:32, :LOW] - v[32:64, LOW:]
        a_im = v[0:32, LOW:] + v[32:64, :LOW]
        b_re = v[64:96, :LOW] - v[96:128, LOW:]
        b_im = v[64:96, LOW:] + v[96:128, :LOW]
        for h, s_re, s_im in ((4 + g, a_re - b_im, a_im + b_re), (3 - g, a_re + b_im, a_im - b_re)):
            cols = slice(128 * h, 128 * h + 128)
            d = -2.0 * (u_ref[0:32, cols] * s_im + u_ref[32:64, cols] * s_re)
            out_ref[2 * h] = jnp.concatenate([d[:16, :64], d[16:, :64]], 1)
            out_ref[2 * h + 1] = jnp.concatenate([d[:16, 64:], d[16:, 64:]], 1)


def pack(block):
    return jnp.concatenate([block[:16], block[16:]], 1)


def shards(theta, panel_rows, point_rows, point_cols, direct, noise):
    points = point_rows.shape[0]
    peers = lax.axis_size("pts")
    elems = lax.axis_size("elem")
    params = pltpu.CompilerParams(vmem_limit_bytes=40 << 20)
    sent = jnp.broadcast_to(pack(theta)[None], (peers, 16, 128))
    angles = lax.all_to_all(sent, "pts", 0, 0, tiled=True)
    prow = point_rows.reshape(CHUNKS, CW)
    pcol = point_cols.reshape(CHUNKS, CW)
    direct = direct.reshape(8, CW)
    noise = noise.reshape(CHUNKS, CW)
    low, high, beam = pl.pallas_call(
        table_kernel,
        out_shape=(
            jax.ShapeDtypeStruct((4 * LOW, points), BF16),
            jax.ShapeDtypeStruct((8, points), F32),
            jax.ShapeDtypeStruct((64, points), F32),
        ),
        compiler_params=params,
        name="tables",
    )(prow, pcol, panel_rows.reshape(32, 1))
    part, phasors = pl.pallas_call(
        field_kernel,
        out_shape=(
            jax.ShapeDtypeStruct((8, CW), F32),
            jax.ShapeDtypeStruct((64, NY_EL), F32),
        ),
        compiler_params=params,
        name="field",
    )(angles, low, high, beam)
    part, direct, noise = lax.optimization_barrier((part, direct, noise))
    parts = lax.all_to_all(jnp.broadcast_to(part[None], (elems, 8, CW)), "elem", 0, 0, tiled=True)
    field, grads = pl.pallas_call(
        gradient_kernel,
        out_shape=(
            jax.ShapeDtypeStruct((8, CW), F32),
            jax.ShapeDtypeStruct((peers, 16, 128), F32),
        ),
        scratch_shapes=[pltpu.VMEM((512, points), BF16), pltpu.VMEM((512, points), BF16)],
        compiler_params=params,
        name="gradient",
    )(parts, direct, noise, prow, pcol, low, high, beam, phasors)
    field, grads = lax.optimization_barrier((field.reshape(2, points), grads))
    total = jnp.sum(lax.all_to_all(grads, "pts", 0, 0, tiled=True), 0)
    grad = jnp.concatenate([total[:, :64], total[:, 64:]], 0)
    return grad, field


def solution(mesh):
    in_specs = (P("elem", "pts"), P("elem"), P("pts"), P("pts"), P(None, "pts"), P("pts"))
    out_specs = (P("elem", "pts"), P(None, "pts"))
    return jax.shard_map(shards, mesh=mesh, in_specs=in_specs, out_specs=out_specs, check_vma=False)
```

```python
import math

import jax
import jax.numpy as jnp
from jax import lax
from jax.experimental import pallas as pl
from jax.experimental.pallas import tpu as pltpu
from jax.sharding import PartitionSpec as P

NX_EL = 1024
NY_EL = 1024
CHUNKS = 4
CW = 512
TURN_IN = 10
TURN_OUT = 10
LOW = 128
TWO_PI = 2.0 * math.pi

F32 = jnp.float32
BF16 = jnp.bfloat16


def _fit(func, degree):
    import numpy as np

    nodes = 0.125 + 0.125 * np.cos(np.pi * (np.arange(64) + 0.5) / 64)
    poly = np.polynomial.Chebyshev.fit(nodes, func(np.sqrt(nodes)), degree, domain=[0.0, 0.25])
    return [float(c) for c in poly.convert(kind=np.polynomial.Polynomial).coef]


def _tables():
    import numpy as np

    return (
        _fit(lambda r: np.sin(np.pi * r) / r, 5),
        _fit(lambda r: np.cos(np.pi * r), 5),
    )


SIN_C, COS_C = _tables()


def _horner(x, coefs):
    acc = jnp.full_like(x, coefs[-1])
    for c in coefs[-2::-1]:
        acc = acc * x + c
    return acc


def cos_sin_turns(t):
    r = t - jnp.round(t)
    x = r * r
    s = r * _horner(x, SIN_C)
    c = _horner(x, COS_C)
    two_s = s + s
    return 1.0 - two_s * s, two_s * c


def split(x):
    hi = x.astype(BF16)
    lo = (x - hi.astype(F32)).astype(BF16)
    return hi, lo


def mm(a, b):
    return lax.dot_general(a, b, (((1,), (0,)), ((), ())), preferred_element_type=F32)


def mm_nt(a, b):
    return lax.dot_general(a, b, (((1,), (1,)), ((), ())), preferred_element_type=F32)


def flip(x):
    i = lax.broadcasted_iota(jnp.int32, (LOW, LOW), 0)
    j = lax.broadcasted_iota(jnp.int32, (LOW, LOW), 1)
    anti = jnp.where(i + j == LOW - 1, 1.0, 0.0).astype(BF16)
    hi, lo = split(x)
    r = mm(jnp.concatenate([hi, lo], 0), anti)
    return r[: x.shape[0]] + r[x.shape[0] :]


def slopes(rows_ref, cols_ref):
    along_x = (rows_ref[...].astype(F32) - 255.5) * 0.5
    along_y = (cols_ref[...].astype(F32) - 127.5) * 0.5
    radius = jnp.sqrt(along_x * along_x + along_y * along_y + 1600.0)
    return along_x / radius, along_y / radius, 80.0 / (radius * 1024.0)


def sides(v):
    out = []
    for h in range(NY_EL // LOW):
        a = v[(2 * h - TURN_IN) % 16]
        b = v[(2 * h + 1 - TURN_IN) % 16]
        top = jnp.concatenate([a[:, :64], b[:, :64]], 1)
        low = jnp.concatenate([a[:, 64:], b[:, 64:]], 1)
        out.append(jnp.concatenate([top, low], 0))
    return out


def pack_kernel(theta_ref, out_ref):
    v = theta_ref[...]
    v = jnp.concatenate([v[:16], v[16:]], 1)
    for z in range(out_ref.shape[0]):
        out_ref[z] = v


def table_kernel(prow_ref, pcol_ref, rows_ref, low_ref, high_ref, x_ref):
    sx, sy, _ = slopes(prow_ref, pcol_ref)
    sx = sx * 0.5
    sy = sy * 0.5
    low_k = lax.broadcasted_iota(jnp.int32, (LOW, CW), 0).astype(F32) + 0.5
    high_k = (lax.broadcasted_iota(jnp.int32, (8, CW), 0) * (2 * LOW)).astype(F32) + LOW
    lattice_x = rows_ref[...].astype(F32) - (NX_EL - 1) / 2.0
    for r in range(CHUNKS):
        cols = slice(CW * r, CW * r + CW)
        c, s = cos_sin_turns(low_k * sy[r : r + 1])
        hi, lo = split(c)
        low_ref[0:LOW, cols] = hi
        low_ref[2 * LOW : 3 * LOW, cols] = lo
        hi, lo = split(s)
        low_ref[LOW : 2 * LOW, cols] = hi
        low_ref[3 * LOW : 4 * LOW, cols] = lo
        c, s = cos_sin_turns(high_k * sy[r : r + 1])
        high_ref[0:4, cols] = c[0:4]
        high_ref[4:8, cols] = s[0:4]
        c, s = cos_sin_turns(lattice_x * sx[r : r + 1])
        x_ref[0:32, cols] = c
        x_ref[32:64, cols] = s


def field_kernel(theta_ref, low_ref, high_ref, x_ref, part_ref, u_ref):
    c, s = cos_sin_turns(theta_ref[...] * (1.0 / TWO_PI))
    re = sides(c)
    im = sides(s)
    back = flip(jnp.concatenate([re[0], im[0], re[2], im[2], re[4], im[4], re[6], im[6]], 0))
    even_re, even_im, odd_re, odd_im = [], [], [], []
    for h in range(4):
        m_re = back[64 * h : 64 * h + 32]
        m_im = back[64 * h + 32 : 64 * h + 64]
        p_re = re[2 * h + 1]
        p_im = im[2 * h + 1]
        cols = slice(LOW * 2 * h, LOW * 2 * h + LOW)
        u_ref[0:32, cols] = m_re
        u_ref[32:64, cols] = m_im
        cols = slice(LOW * (2 * h + 1), LOW * (2 * h + 2))
        u_ref[0:32, cols] = p_re
        u_ref[32:64, cols] = p_im
        even_re.append(p_re + m_re)
        even_im.append(p_im + m_im)
        odd_re.append(p_re - m_re)
        odd_im.append(p_im - m_im)
    rows = []
    for g in range(2):
        for sign in (1.0, -1.0):
            e_re, e_im, o_re, o_im = (v[2 + g] + sign * v[1 - g] for v in (even_re, even_im, odd_re, odd_im))
            rows.append(jnp.concatenate([e_re, -o_im], 1))
            rows.append(jnp.concatenate([e_im, o_re], 1))
    hi, lo = split(jnp.concatenate(rows, 0))
    left = jnp.concatenate([hi, hi, lo], 1)
    for r in range(CHUNKS):
        cols = slice(CW * r, CW * r + CW)
        p = mm(left, jnp.concatenate([low_ref[:, cols], low_ref[0 : 2 * LOW, cols]], 0))
        f_re = jnp.zeros((32, CW), F32)
        f_im = jnp.zeros((32, CW), F32)
        for g in range(2):
            hc = high_ref[g : g + 1, cols]
            hs = high_ref[4 + g : 5 + g, cols]
            q = p[128 * g : 128 * g + 128]
            f_re = f_re + (hc * q[0:32] - hs * q[96:128])
            f_im = f_im + (hc * q[32:64] + hs * q[64:96])
        xc = x_ref[0:32, cols]
        xs = x_ref[32:64, cols]
        part_ref[r : r + 1] = jnp.sum(xc * f_re - xs * f_im, 0, keepdims=True)
        part_ref[r + 4 : r + 5] = jnp.sum(xc * f_im + xs * f_re, 0, keepdims=True)


def gradient_kernel(
    parts_ref, direct_ref, noise_ref, prow_ref, pcol_ref, low_ref, high_ref, x_ref, u_ref, field_ref, out_ref, held_ref, whi_ref, wlo_ref, sem
):
    _, _, scale = slopes(prow_ref, pcol_ref)
    total = jnp.sum(parts_ref[...], 0)
    re = direct_ref[0:4] + scale * total[0:4]
    im = direct_ref[4:8] + scale * total[4:8]
    for r in range(CHUNKS):
        cols = slice(CW * r, CW * r + CW)
        held_ref[0:1, cols] = re[r : r + 1]
        held_ref[1:2, cols] = im[r : r + 1]
    copy = pltpu.make_async_copy(held_ref, field_ref, sem)
    copy.start()
    power = noise_ref[...] + re * re + im * im
    q_re = re * scale / power
    q_im = -im * scale / power
    for r in range(CHUNKS):
        cols = slice(CW * r, CW * r + CW)
        a = q_re[r : r + 1]
        b = q_im[r : r + 1]
        xc = x_ref[0:32, cols]
        xs = x_ref[32:64, cols]
        w_re = a * xc - b * xs
        w_im = a * xs + b * xc
        w = jnp.concatenate([w_re, w_im], 0)
        for g in range(2):
            hi, lo = split(w * high_ref[g : g + 1, cols])
            whi_ref[128 * g : 128 * g + 64, cols] = hi
            wlo_ref[128 * g : 128 * g + 64, cols] = lo
            hi, lo = split(w * high_ref[4 + g : 5 + g, cols])
            whi_ref[128 * g + 64 : 128 * g + 128, cols] = hi
            wlo_ref[128 * g + 64 : 128 * g + 128, cols] = lo
    sums = (
        mm_nt(whi_ref[...], low_ref[0 : 2 * LOW])
        + mm_nt(wlo_ref[...], low_ref[0 : 2 * LOW])
        + mm_nt(whi_ref[...], low_ref[2 * LOW :])
    )
    blocks = [None] * 8
    for g in range(2):
        v = sums[128 * g : 128 * g + 128]
        cc = v[0:64, :LOW]
        cs = v[0:64, LOW:]
        sc = v[64:128, :LOW]
        ss = v[64:128, LOW:]
        minus = cc - ss
        plus = cc + ss
        added = cs + sc
        taken = cs - sc
        for n, real, imag in (
            (5 + 2 * g, minus, added),
            (4 + 2 * g, plus, -taken),
            (3 - 2 * g, plus, taken),
            (2 - 2 * g, minus, -added),
        ):
            s_re = real[:32] - imag[32:]
            s_im = real[32:] + imag[:32]
            cols = slice(LOW * n, LOW * n + LOW)
            blocks[n] = -2.0 * (u_ref[0:32, cols] * s_im + u_ref[32:64, cols] * s_re)
    back = flip(jnp.concatenate(blocks[0::2], 0))
    for n in range(8):
        d = blocks[n] if n % 2 else back[16 * n : 16 * n + 32]
        out_ref[(2 * n - TURN_OUT) % 16] = jnp.concatenate([d[:16, :64], d[16:, :64]], 1)
        out_ref[(2 * n + 1 - TURN_OUT) % 16] = jnp.concatenate([d[:16, 64:], d[16:, 64:]], 1)
    copy.wait()


def shards(theta, panel_rows, point_rows, point_cols, direct, noise):
    points = point_rows.shape[0]
    peers = lax.axis_size("pts")
    elems = lax.axis_size("elem")
    params = pltpu.CompilerParams(vmem_limit_bytes=40 << 20)
    sent = pl.pallas_call(
        pack_kernel,
        out_shape=jax.ShapeDtypeStruct((peers, 16, 128), F32),
        compiler_params=params,
        name="pack",
    )(theta)
    along_in = [[(i + TURN_IN) % peers for i in range(peers)]]
    along_out = [[(i + TURN_OUT) % peers for i in range(peers)]]
    plane = [[(i + 21) % elems for i in range(elems)]]
    angles = lax.all_to_all(sent, "pts", 0, 0, axis_index_groups=along_in, tiled=True)
    prow = point_rows.reshape(CHUNKS, CW)
    pcol = point_cols.reshape(CHUNKS, CW)
    direct = direct.reshape(8, CW)
    noise = noise.reshape(CHUNKS, CW)
    low, high, beam = pl.pallas_call(
        table_kernel,
        out_shape=(
            jax.ShapeDtypeStruct((4 * LOW, points), BF16),
            jax.ShapeDtypeStruct((8, points), F32),
            jax.ShapeDtypeStruct((64, points), F32),
        ),
        compiler_params=params,
        name="tables",
    )(prow, pcol, panel_rows.reshape(32, 1))
    part, phasors = pl.pallas_call(
        field_kernel,
        out_shape=(
            jax.ShapeDtypeStruct((8, CW), F32),
            jax.ShapeDtypeStruct((64, NY_EL), F32),
        ),
        compiler_params=params,
        name="field",
    )(angles, low, high, beam)
    part, direct, noise = lax.optimization_barrier((part, direct, noise))
    parts = lax.all_to_all(jnp.broadcast_to(part[None], (elems, 8, CW)), "elem", 0, 0, axis_index_groups=plane, tiled=True)
    field, grads = pl.pallas_call(
        gradient_kernel,
        out_shape=(
            jax.ShapeDtypeStruct((2, points), F32),
            jax.ShapeDtypeStruct((peers, 16, 128), F32),
        ),
        out_specs=(pl.BlockSpec(memory_space=pl.ANY), pl.BlockSpec(memory_space=pltpu.VMEM)),
        scratch_shapes=[
            pltpu.VMEM((2, points), F32),
            pltpu.VMEM((256, points), BF16),
            pltpu.VMEM((256, points), BF16),
            pltpu.SemaphoreType.DMA,
        ],
        compiler_params=params,
        name="gradient",
    )(parts, direct, noise, prow, pcol, low, high, beam, phasors)
    total = jnp.sum(lax.all_to_all(grads, "pts", 0, 0, axis_index_groups=along_out, tiled=True), 0)
    grad = jnp.concatenate([total[:, :64], total[:, 64:]], 0)
    return grad, field


def solution(mesh):
    in_specs = (P("elem", "pts"), P("elem"), P("pts"), P("pts"), P(None, "pts"), P("pts"))
    out_specs = (P("elem", "pts"), P(None, "pts"))
    return jax.shard_map(shards, mesh=mesh, in_specs=in_specs, out_specs=out_specs, check_vma=False)
```

```python
import math

import jax
import jax.numpy as jnp
from jax import lax
from jax.experimental import pallas as pl
from jax.experimental.pallas import tpu as pltpu
from jax.sharding import PartitionSpec as P

NX_EL = 1024
NY_EL = 1024
CHUNKS = 4
CW = 512
TURN_IN = 10
TURN_OUT = 10
LOW = 128
TWO_PI = 2.0 * math.pi

F32 = jnp.float32
BF16 = jnp.bfloat16


def _fit(func, degree):
    import numpy as np

    nodes = 0.125 + 0.125 * np.cos(np.pi * (np.arange(64) + 0.5) / 64)
    poly = np.polynomial.Chebyshev.fit(nodes, func(np.sqrt(nodes)), degree, domain=[0.0, 0.25])
    return [float(c) for c in poly.convert(kind=np.polynomial.Polynomial).coef]


def _tables():
    import numpy as np

    return (
        _fit(lambda r: np.sin(np.pi * r) / r, 5),
        _fit(lambda r: np.cos(np.pi * r), 5),
    )


SIN_C, COS_C = _tables()


def _horner(x, coefs):
    acc = jnp.full_like(x, coefs[-1])
    for c in coefs[-2::-1]:
        acc = acc * x + c
    return acc


def cos_sin_turns(t):
    r = t - jnp.round(t)
    x = r * r
    s = r * _horner(x, SIN_C)
    c = _horner(x, COS_C)
    two_s = s + s
    return 1.0 - two_s * s, two_s * c


def split(x):
    hi = x.astype(BF16)
    lo = (x - hi.astype(F32)).astype(BF16)
    return hi, lo


def mm(a, b):
    return lax.dot_general(a, b, (((1,), (0,)), ((), ())), preferred_element_type=F32)


def mm_nt(a, b):
    return lax.dot_general(a, b, (((1,), (1,)), ((), ())), preferred_element_type=F32)


def flip(x):
    i = lax.broadcasted_iota(jnp.int32, (LOW, LOW), 0)
    j = lax.broadcasted_iota(jnp.int32, (LOW, LOW), 1)
    anti = jnp.where(i + j == LOW - 1, 1.0, 0.0).astype(BF16)
    hi, lo = split(x)
    r = mm(jnp.concatenate([hi, lo], 0), anti)
    return r[: x.shape[0]] + r[x.shape[0] :]


def slopes(rows_ref, cols_ref):
    along_x = (rows_ref[...].astype(F32) - 255.5) * 0.5
    along_y = (cols_ref[...].astype(F32) - 127.5) * 0.5
    radius = jnp.sqrt(along_x * along_x + along_y * along_y + 1600.0)
    return along_x / radius, along_y / radius, 80.0 / (radius * 1024.0)


def sides(v):
    out = []
    for h in range(NY_EL // LOW):
        a = v[(2 * h - TURN_IN) % 16]
        b = v[(2 * h + 1 - TURN_IN) % 16]
        top = jnp.concatenate([a[:, :64], b[:, :64]], 1)
        low = jnp.concatenate([a[:, 64:], b[:, 64:]], 1)
        out.append(jnp.concatenate([top, low], 0))
    return out


def pack_kernel(theta_ref, out_ref, in_ref, held_ref, sems):
    fetch = pltpu.make_async_copy(theta_ref, in_ref, sems.at[0])
    fetch.start()
    fetch.wait()
    v = in_ref[...]
    v = jnp.concatenate([v[:16], v[16:]], 1)
    for z in range(out_ref.shape[0]):
        held_ref[z] = v
    store = pltpu.make_async_copy(held_ref, out_ref, sems.at[1])
    store.start()
    store.wait()


def table_kernel(prow_ref, pcol_ref, rows_ref, low_ref, high_ref, x_ref):
    sx, sy, _ = slopes(prow_ref, pcol_ref)
    sx = sx * 0.5
    sy = sy * 0.5
    low_k = lax.broadcasted_iota(jnp.int32, (LOW, CW), 0).astype(F32) + 0.5
    high_k = (lax.broadcasted_iota(jnp.int32, (8, CW), 0) * (2 * LOW)).astype(F32) + LOW
    lattice_x = rows_ref[...].astype(F32) - (NX_EL - 1) / 2.0
    for r in range(CHUNKS):
        cols = slice(CW * r, CW * r + CW)
        c, s = cos_sin_turns(low_k * sy[r : r + 1])
        hi, lo = split(c)
        low_ref[0:LOW, cols] = hi
        low_ref[2 * LOW : 3 * LOW, cols] = lo
        hi, lo = split(s)
        low_ref[LOW : 2 * LOW, cols] = hi
        low_ref[3 * LOW : 4 * LOW, cols] = lo
        c, s = cos_sin_turns(high_k * sy[r : r + 1])
        high_ref[0:4, cols] = c[0:4]
        high_ref[4:8, cols] = s[0:4]
        c, s = cos_sin_turns(lattice_x * sx[r : r + 1])
        x_ref[0:32, cols] = c
        x_ref[32:64, cols] = s


def field_kernel(theta_ref, low_ref, high_ref, x_ref, part_ref, u_ref):
    c, s = cos_sin_turns(theta_ref[...] * (1.0 / TWO_PI))
    re = sides(c)
    im = sides(s)
    back = flip(jnp.concatenate([re[0], im[0], re[2], im[2], re[4], im[4], re[6], im[6]], 0))
    even_re, even_im, odd_re, odd_im = [], [], [], []
    for h in range(4):
        m_re = back[64 * h : 64 * h + 32]
        m_im = back[64 * h + 32 : 64 * h + 64]
        p_re = re[2 * h + 1]
        p_im = im[2 * h + 1]
        cols = slice(LOW * 2 * h, LOW * 2 * h + LOW)
        u_ref[0:32, cols] = m_re
        u_ref[32:64, cols] = m_im
        cols = slice(LOW * (2 * h + 1), LOW * (2 * h + 2))
        u_ref[0:32, cols] = p_re
        u_ref[32:64, cols] = p_im
        even_re.append(p_re + m_re)
        even_im.append(p_im + m_im)
        odd_re.append(p_re - m_re)
        odd_im.append(p_im - m_im)
    rows = []
    for g in range(2):
        for sign in (1.0, -1.0):
            e_re, e_im, o_re, o_im = (v[2 + g] + sign * v[1 - g] for v in (even_re, even_im, odd_re, odd_im))
            rows.append(jnp.concatenate([e_re, -o_im], 1))
            rows.append(jnp.concatenate([e_im, o_re], 1))
    hi, lo = split(jnp.concatenate(rows, 0))
    left = jnp.concatenate([hi, hi, lo], 1)
    for r in range(CHUNKS):
        cols = slice(CW * r, CW * r + CW)
        p = mm(left, jnp.concatenate([low_ref[:, cols], low_ref[0 : 2 * LOW, cols]], 0))
        f_re = jnp.zeros((32, CW), F32)
        f_im = jnp.zeros((32, CW), F32)
        for g in range(2):
            hc = high_ref[g : g + 1, cols]
            hs = high_ref[4 + g : 5 + g, cols]
            q = p[128 * g : 128 * g + 128]
            f_re = f_re + (hc * q[0:32] - hs * q[96:128])
            f_im = f_im + (hc * q[32:64] + hs * q[64:96])
        xc = x_ref[0:32, cols]
        xs = x_ref[32:64, cols]
        part_ref[r : r + 1] = jnp.sum(xc * f_re - xs * f_im, 0, keepdims=True)
        part_ref[r + 4 : r + 5] = jnp.sum(xc * f_im + xs * f_re, 0, keepdims=True)


def gradient_kernel(
    parts_ref, direct_ref, noise_ref, prow_ref, pcol_ref, low_ref, high_ref, x_ref, u_ref, field_ref, out_ref, held_ref, w_ref, sem
):
    _, _, scale = slopes(prow_ref, pcol_ref)
    total = jnp.sum(parts_ref[...], 0)
    re = direct_ref[0:4] + scale * total[0:4]
    im = direct_ref[4:8] + scale * total[4:8]
    for r in range(CHUNKS):
        cols = slice(CW * r, CW * r + CW)
        held_ref[0:1, cols] = re[r : r + 1]
        held_ref[1:2, cols] = im[r : r + 1]
    copy = pltpu.make_async_copy(held_ref, field_ref, sem)
    copy.start()
    power = noise_ref[...] + re * re + im * im
    q_re = re * scale / power
    q_im = -im * scale / power
    for r in range(CHUNKS):
        cols = slice(CW * r, CW * r + CW)
        a = q_re[r : r + 1]
        b = q_im[r : r + 1]
        xc = x_ref[0:32, cols]
        xs = x_ref[32:64, cols]
        w_re = a * xc - b * xs
        w_im = a * xs + b * xc
        w = jnp.concatenate([w_re, w_im], 0)
        for g in range(2):
            hi, lo = split(w * high_ref[g : g + 1, cols])
            w_ref[128 * g : 128 * g + 64, cols] = hi
            w_ref[256 + 128 * g : 320 + 128 * g, cols] = lo
            hi, lo = split(w * high_ref[4 + g : 5 + g, cols])
            w_ref[128 * g + 64 : 128 * g + 128, cols] = hi
            w_ref[320 + 128 * g : 384 + 128 * g, cols] = lo
    first = mm_nt(w_ref[...], low_ref[0 : 2 * LOW])
    sums = first[:256] + first[256:] + mm_nt(w_ref[0:256], low_ref[2 * LOW :])
    blocks = [None] * 8
    for g in range(2):
        v = sums[128 * g : 128 * g + 128]
        cc = v[0:64, :LOW]
        cs = v[0:64, LOW:]
        sc = v[64:128, :LOW]
        ss = v[64:128, LOW:]
        minus = cc - ss
        plus = cc + ss
        added = cs + sc
        taken = cs - sc
        for n, real, imag in (
            (5 + 2 * g, minus, added),
            (4 + 2 * g, plus, -taken),
            (3 - 2 * g, plus, taken),
            (2 - 2 * g, minus, -added),
        ):
            s_re = real[:32] - imag[32:]
            s_im = real[32:] + imag[:32]
            cols = slice(LOW * n, LOW * n + LOW)
            blocks[n] = -2.0 * (u_ref[0:32, cols] * s_im + u_ref[32:64, cols] * s_re)
    back = flip(jnp.concatenate(blocks[0::2], 0))
    for n in range(8):
        d = blocks[n] if n % 2 else back[16 * n : 16 * n + 32]
        out_ref[(2 * n - TURN_OUT) % 16] = jnp.concatenate([d[:16, :64], d[16:, :64]], 1)
        out_ref[(2 * n + 1 - TURN_OUT) % 16] = jnp.concatenate([d[:16, 64:], d[16:, 64:]], 1)
    copy.wait()


def shards(theta, panel_rows, point_rows, point_cols, direct, noise):
    points = point_rows.shape[0]
    peers = lax.axis_size("pts")
    elems = lax.axis_size("elem")
    params = pltpu.CompilerParams(vmem_limit_bytes=40 << 20)
    sent = pl.pallas_call(
        pack_kernel,
        out_shape=jax.ShapeDtypeStruct((peers, 16, 128), F32),
        in_specs=[pl.BlockSpec(memory_space=pltpu.HBM)],
        out_specs=pl.BlockSpec(memory_space=pltpu.HBM),
        scratch_shapes=[
            pltpu.VMEM(theta.shape, F32),
            pltpu.VMEM((peers, 16, 128), F32),
            pltpu.SemaphoreType.DMA((2,)),
        ],
        compiler_params=params,
        name="pack",
    )(theta)
    along_in = [[(i + TURN_IN) % peers for i in range(peers)]]
    along_out = [[(i + TURN_OUT) % peers for i in range(peers)]]
    plane = [[(2 * i + 20) % elems + core for i in range(elems // 2)] for core in (0, 1)]
    angles = lax.all_to_all(sent, "pts", 0, 0, axis_index_groups=along_in, tiled=True)
    prow = point_rows.reshape(CHUNKS, CW)
    pcol = point_cols.reshape(CHUNKS, CW)
    direct = direct.reshape(8, CW)
    noise = noise.reshape(CHUNKS, CW)
    low, high, beam = pl.pallas_call(
        table_kernel,
        out_shape=(
            jax.ShapeDtypeStruct((4 * LOW, points), BF16),
            jax.ShapeDtypeStruct((8, points), F32),
            jax.ShapeDtypeStruct((64, points), F32),
        ),
        compiler_params=params,
        name="tables",
    )(prow, pcol, panel_rows.reshape(32, 1))
    part, phasors = pl.pallas_call(
        field_kernel,
        out_shape=(
            jax.ShapeDtypeStruct((8, CW), F32),
            jax.ShapeDtypeStruct((64, NY_EL), F32),
        ),
        compiler_params=params,
        name="field",
    )(angles, low, high, beam)
    part, direct, noise = lax.optimization_barrier((part, direct, noise))
    part = part + lax.ppermute(part, "elem", [(i, i ^ 1) for i in range(elems)])
    parts = lax.all_to_all(jnp.broadcast_to(part[None], (elems // 2, 8, CW)), "elem", 0, 0, axis_index_groups=plane, tiled=True)
    field, grads = pl.pallas_call(
        gradient_kernel,
        out_shape=(
            jax.ShapeDtypeStruct((2, points), F32),
            jax.ShapeDtypeStruct((peers, 16, 128), F32),
        ),
        out_specs=(pl.BlockSpec(memory_space=pl.ANY), pl.BlockSpec(memory_space=pltpu.VMEM)),
        scratch_shapes=[
            pltpu.VMEM((2, points), F32),
            pltpu.VMEM((512, points), BF16),
            pltpu.SemaphoreType.DMA,
        ],
        compiler_params=params,
        name="gradient",
    )(parts, direct, noise, prow, pcol, low, high, beam, phasors)
    total = jnp.sum(lax.all_to_all(grads, "pts", 0, 0, axis_index_groups=along_out, tiled=True), 0)
    grad = jnp.concatenate([total[:, :64], total[:, 64:]], 0)
    return grad, field


def solution(mesh):
    in_specs = (P("elem", "pts"), P("elem"), P("pts"), P("pts"), P(None, "pts"), P("pts"))
    out_specs = (P("elem", "pts"), P(None, "pts"))
    return jax.shard_map(shards, mesh=mesh, in_specs=in_specs, out_specs=out_specs, check_vma=False)
```

```python
import math

import jax
import jax.numpy as jnp
from jax import lax
from jax.experimental import pallas as pl
from jax.experimental.pallas import tpu as pltpu
from jax.sharding import PartitionSpec as P

NX_EL = 1024
NY_EL = 1024
CHUNKS = 4
CW = 512
TURN_IN = 10
TURN_OUT = 10
LOW = 128
TWO_PI = 2.0 * math.pi

F32 = jnp.float32
BF16 = jnp.bfloat16


def _fit(func, degree):
    import numpy as np

    nodes = 0.125 + 0.125 * np.cos(np.pi * (np.arange(64) + 0.5) / 64)
    poly = np.polynomial.Chebyshev.fit(nodes, func(np.sqrt(nodes)), degree, domain=[0.0, 0.25])
    return [float(c) for c in poly.convert(kind=np.polynomial.Polynomial).coef]


def _tables():
    import numpy as np

    return (
        _fit(lambda r: np.sin(np.pi * r) / r, 5),
        _fit(lambda r: np.cos(np.pi * r), 5),
    )


SIN_C, COS_C = _tables()


def _horner(x, coefs):
    acc = jnp.full_like(x, coefs[-1])
    for c in coefs[-2::-1]:
        acc = acc * x + c
    return acc


def cos_sin_turns(t):
    r = t - jnp.round(t)
    x = r * r
    s = r * _horner(x, SIN_C)
    c = _horner(x, COS_C)
    two_s = s + s
    return 1.0 - two_s * s, two_s * c


def split(x):
    hi = x.astype(BF16)
    lo = (x - hi.astype(F32)).astype(BF16)
    return hi, lo


def mm(a, b):
    return lax.dot_general(a, b, (((1,), (0,)), ((), ())), preferred_element_type=F32)


def mm_nt(a, b):
    return lax.dot_general(a, b, (((1,), (1,)), ((), ())), preferred_element_type=F32)


def flip(x):
    i = lax.broadcasted_iota(jnp.int32, (LOW, LOW), 0)
    j = lax.broadcasted_iota(jnp.int32, (LOW, LOW), 1)
    anti = jnp.where(i + j == LOW - 1, 1.0, 0.0).astype(BF16)
    hi, lo = split(x)
    r = mm(jnp.concatenate([hi, lo], 0), anti)
    return r[: x.shape[0]] + r[x.shape[0] :]


def slopes(rows_ref, cols_ref):
    along_x = (rows_ref[...].astype(F32) - 255.5) * 0.5
    along_y = (cols_ref[...].astype(F32) - 127.5) * 0.5
    radius = jnp.sqrt(along_x * along_x + along_y * along_y + 1600.0)
    return along_x / radius, along_y / radius, 80.0 / (radius * 1024.0)


def sides(v):
    out = []
    for h in range(NY_EL // LOW):
        a = v[(2 * h - TURN_IN) % 16]
        b = v[(2 * h + 1 - TURN_IN) % 16]
        top = jnp.concatenate([a[:, :64], b[:, :64]], 1)
        low = jnp.concatenate([a[:, 64:], b[:, 64:]], 1)
        out.append(jnp.concatenate([top, low], 0))
    return out


def pack_kernel(theta_ref, out_ref, in_ref, held_ref, sems):
    fetch = pltpu.make_async_copy(theta_ref, in_ref, sems.at[0])
    fetch.start()
    fetch.wait()
    v = in_ref[...]
    v = jnp.concatenate([v[:16], v[16:]], 1)
    for z in range(out_ref.shape[0]):
        held_ref[z] = v
    store = pltpu.make_async_copy(held_ref, out_ref, sems.at[1])
    store.start()
    store.wait()


def table_kernel(prow_ref, pcol_ref, rows_ref, low_ref, high_ref, x_ref):
    sx, sy, _ = slopes(prow_ref, pcol_ref)
    sx = sx * 0.5
    sy = sy * 0.5
    low_k = lax.broadcasted_iota(jnp.int32, (LOW, CW), 0).astype(F32) + 0.5
    high_k = (lax.broadcasted_iota(jnp.int32, (8, CW), 0) * (2 * LOW)).astype(F32) + LOW
    lattice_x = rows_ref[...].astype(F32) - (NX_EL - 1) / 2.0
    for r in range(CHUNKS):
        cols = slice(CW * r, CW * r + CW)
        c, s = cos_sin_turns(low_k * sy[r : r + 1])
        hi, lo = split(c)
        low_ref[0:LOW, cols] = hi
        low_ref[2 * LOW : 3 * LOW, cols] = lo
        hi, lo = split(s)
        low_ref[LOW : 2 * LOW, cols] = hi
        low_ref[3 * LOW : 4 * LOW, cols] = lo
        c, s = cos_sin_turns(high_k * sy[r : r + 1])
        high_ref[0:4, cols] = c[0:4]
        high_ref[4:8, cols] = s[0:4]
        c, s = cos_sin_turns(lattice_x * sx[r : r + 1])
        x_ref[0:32, cols] = c
        x_ref[32:64, cols] = s


def field_kernel(theta_ref, low_ref, high_ref, x_ref, part_ref, u_ref):
    c, s = cos_sin_turns(theta_ref[...] * (1.0 / TWO_PI))
    re = sides(c)
    im = sides(s)
    back = flip(jnp.concatenate([re[0], im[0], re[2], im[2], re[4], im[4], re[6], im[6]], 0))
    even_re, even_im, odd_re, odd_im = [], [], [], []
    for h in range(4):
        m_re = back[64 * h : 64 * h + 32]
        m_im = back[64 * h + 32 : 64 * h + 64]
        p_re = re[2 * h + 1]
        p_im = im[2 * h + 1]
        cols = slice(LOW * 2 * h, LOW * 2 * h + LOW)
        u_ref[0:32, cols] = m_re
        u_ref[32:64, cols] = m_im
        cols = slice(LOW * (2 * h + 1), LOW * (2 * h + 2))
        u_ref[0:32, cols] = p_re
        u_ref[32:64, cols] = p_im
        even_re.append(p_re + m_re)
        even_im.append(p_im + m_im)
        odd_re.append(p_re - m_re)
        odd_im.append(p_im - m_im)
    rows = []
    for g in range(2):
        for sign in (1.0, -1.0):
            e_re, e_im, o_re, o_im = (v[2 + g] + sign * v[1 - g] for v in (even_re, even_im, odd_re, odd_im))
            rows.append(jnp.concatenate([e_re, -o_im], 1))
            rows.append(jnp.concatenate([e_im, o_re], 1))
    hi, lo = split(jnp.concatenate(rows, 0))
    left = jnp.concatenate([hi, hi, lo], 1)
    for r in range(CHUNKS):
        cols = slice(CW * r, CW * r + CW)
        p = mm(left, jnp.concatenate([low_ref[:, cols], low_ref[0 : 2 * LOW, cols]], 0))
        f_re = jnp.zeros((32, CW), F32)
        f_im = jnp.zeros((32, CW), F32)
        for g in range(2):
            hc = high_ref[g : g + 1, cols]
            hs = high_ref[4 + g : 5 + g, cols]
            q = p[128 * g : 128 * g + 128]
            f_re = f_re + (hc * q[0:32] - hs * q[96:128])
            f_im = f_im + (hc * q[32:64] + hs * q[64:96])
        xc = x_ref[0:32, cols]
        xs = x_ref[32:64, cols]
        part_ref[r : r + 1] = jnp.sum(xc * f_re - xs * f_im, 0, keepdims=True)
        part_ref[r + 4 : r + 5] = jnp.sum(xc * f_im + xs * f_re, 0, keepdims=True)


def gradient_kernel(
    parts_ref, direct_ref, noise_ref, prow_ref, pcol_ref, low_ref, high_ref, x_ref, u_ref, field_ref, out_ref, w_ref
):
    _, _, scale = slopes(prow_ref, pcol_ref)
    total = jnp.sum(parts_ref[...], 0)
    re = direct_ref[0:4] + scale * total[0:4]
    im = direct_ref[4:8] + scale * total[4:8]
    field_ref[0:4] = re
    field_ref[4:8] = im
    power = noise_ref[...] + re * re + im * im
    q_re = re * scale / power
    q_im = -im * scale / power
    for r in range(CHUNKS):
        cols = slice(CW * r, CW * r + CW)
        a = q_re[r : r + 1]
        b = q_im[r : r + 1]
        xc = x_ref[0:32, cols]
        xs = x_ref[32:64, cols]
        w_re = a * xc - b * xs
        w_im = a * xs + b * xc
        w = jnp.concatenate([w_re, w_im], 0)
        for g in range(2):
            hi, lo = split(w * high_ref[g : g + 1, cols])
            w_ref[128 * g : 128 * g + 64, cols] = hi
            w_ref[256 + 128 * g : 320 + 128 * g, cols] = lo
            hi, lo = split(w * high_ref[4 + g : 5 + g, cols])
            w_ref[128 * g + 64 : 128 * g + 128, cols] = hi
            w_ref[320 + 128 * g : 384 + 128 * g, cols] = lo
    first = mm_nt(w_ref[...], low_ref[0 : 2 * LOW])
    sums = first[:256] + first[256:] + mm_nt(w_ref[0:256], low_ref[2 * LOW :])
    blocks = [None] * 8
    for g in range(2):
        v = sums[128 * g : 128 * g + 128]
        cc = v[0:64, :LOW]
        cs = v[0:64, LOW:]
        sc = v[64:128, :LOW]
        ss = v[64:128, LOW:]
        minus = cc - ss
        plus = cc + ss
        added = cs + sc
        taken = cs - sc
        for n, real, imag in (
            (5 + 2 * g, minus, added),
            (4 + 2 * g, plus, -taken),
            (3 - 2 * g, plus, taken),
            (2 - 2 * g, minus, -added),
        ):
            s_re = real[:32] - imag[32:]
            s_im = real[32:] + imag[:32]
            cols = slice(LOW * n, LOW * n + LOW)
            blocks[n] = -2.0 * (u_ref[0:32, cols] * s_im + u_ref[32:64, cols] * s_re)
    back = flip(jnp.concatenate(blocks[0::2], 0))
    for n in range(8):
        d = blocks[n] if n % 2 else back[16 * n : 16 * n + 32]
        out_ref[(2 * n - TURN_OUT) % 16] = jnp.concatenate([d[:16, :64], d[16:, :64]], 1)
        out_ref[(2 * n + 1 - TURN_OUT) % 16] = jnp.concatenate([d[:16, 64:], d[16:, 64:]], 1)


def last_kernel(got_ref, held_ref, grad_ref, field_ref):
    total = jnp.sum(got_ref[...], 0)
    grad_ref[0:16] = total[:, :64]
    grad_ref[16:32] = total[:, 64:]
    for r in range(CHUNKS):
        cols = slice(CW * r, CW * r + CW)
        field_ref[0:1, cols] = held_ref[r : r + 1]
        field_ref[1:2, cols] = held_ref[r + 4 : r + 5]


def shards(theta, panel_rows, point_rows, point_cols, direct, noise):
    points = point_rows.shape[0]
    peers = lax.axis_size("pts")
    elems = lax.axis_size("elem")
    params = pltpu.CompilerParams(vmem_limit_bytes=40 << 20)
    sent = pl.pallas_call(
        pack_kernel,
        out_shape=jax.ShapeDtypeStruct((peers, 16, 128), F32),
        in_specs=[pl.BlockSpec(memory_space=pltpu.HBM)],
        out_specs=pl.BlockSpec(memory_space=pltpu.HBM),
        scratch_shapes=[
            pltpu.VMEM(theta.shape, F32),
            pltpu.VMEM((peers, 16, 128), F32),
            pltpu.SemaphoreType.DMA((2,)),
        ],
        compiler_params=params,
        name="pack",
    )(theta)
    along_in = [[(i + TURN_IN) % peers for i in range(peers)]]
    along_out = [[(i + TURN_OUT) % peers for i in range(peers)]]
    plane = [[(2 * i + 20) % elems + core for i in range(elems // 2)] for core in (0, 1)]
    angles = lax.all_to_all(sent, "pts", 0, 0, axis_index_groups=along_in, tiled=True)
    prow = point_rows.reshape(CHUNKS, CW)
    pcol = point_cols.reshape(CHUNKS, CW)
    direct = direct.reshape(8, CW)
    noise = noise.reshape(CHUNKS, CW)
    low, high, beam = pl.pallas_call(
        table_kernel,
        out_shape=(
            jax.ShapeDtypeStruct((4 * LOW, points), BF16),
            jax.ShapeDtypeStruct((8, points), F32),
            jax.ShapeDtypeStruct((64, points), F32),
        ),
        compiler_params=params,
        name="tables",
    )(prow, pcol, panel_rows.reshape(32, 1))
    part, phasors = pl.pallas_call(
        field_kernel,
        out_shape=(
            jax.ShapeDtypeStruct((8, CW), F32),
            jax.ShapeDtypeStruct((64, NY_EL), F32),
        ),
        compiler_params=params,
        name="field",
    )(angles, low, high, beam)
    part, direct, noise = lax.optimization_barrier((part, direct, noise))
    part = part + lax.ppermute(part, "elem", [(i, i ^ 1) for i in range(elems)])
    parts = lax.all_to_all(jnp.broadcast_to(part[None], (elems // 2, 8, CW)), "elem", 0, 0, axis_index_groups=plane, tiled=True)
    field, grads = pl.pallas_call(
        gradient_kernel,
        out_shape=(
            jax.ShapeDtypeStruct((8, CW), F32),
            jax.ShapeDtypeStruct((peers, 16, 128), F32),
        ),
        scratch_shapes=[pltpu.VMEM((512, points), BF16)],
        compiler_params=params,
        name="gradient",
    )(parts, direct, noise, prow, pcol, low, high, beam, phasors)
    got = lax.all_to_all(grads, "pts", 0, 0, axis_index_groups=along_out, tiled=True)
    return pl.pallas_call(
        last_kernel,
        out_shape=(
            jax.ShapeDtypeStruct(theta.shape, F32),
            jax.ShapeDtypeStruct((2, points), F32),
        ),
        compiler_params=params,
        name="last",
    )(got, field)


def solution(mesh):
    in_specs = (P("elem", "pts"), P("elem"), P("pts"), P("pts"), P(None, "pts"), P("pts"))
    out_specs = (P("elem", "pts"), P(None, "pts"))
    return jax.shard_map(shards, mesh=mesh, in_specs=in_specs, out_specs=out_specs, check_vma=False)
```

```python
import math

import jax
import jax.numpy as jnp
from jax import lax
from jax.experimental import pallas as pl
from jax.experimental.pallas import tpu as pltpu
from jax.sharding import PartitionSpec as P

NX_EL = 1024
NY_EL = 1024
CHUNKS = 4
CW = 512
TURN_IN = 10
TURN_OUT = 10
LOW = 128
TWO_PI = 2.0 * math.pi

F32 = jnp.float32
BF16 = jnp.bfloat16


def _fit(func, degree):
    import numpy as np

    nodes = 0.125 + 0.125 * np.cos(np.pi * (np.arange(64) + 0.5) / 64)
    poly = np.polynomial.Chebyshev.fit(nodes, func(np.sqrt(nodes)), degree, domain=[0.0, 0.25])
    return [float(c) for c in poly.convert(kind=np.polynomial.Polynomial).coef]


def _tables():
    import numpy as np

    return (
        _fit(lambda r: np.sin(np.pi * r) / r, 5),
        _fit(lambda r: np.cos(np.pi * r), 5),
    )


SIN_C, COS_C = _tables()


def _horner(x, coefs):
    acc = jnp.full_like(x, coefs[-1])
    for c in coefs[-2::-1]:
        acc = acc * x + c
    return acc


def cos_sin_turns(t):
    r = t - jnp.round(t)
    x = r * r
    s = r * _horner(x, SIN_C)
    c = _horner(x, COS_C)
    two_s = s + s
    return 1.0 - two_s * s, two_s * c


def split(x):
    hi = x.astype(BF16)
    lo = (x - hi.astype(F32)).astype(BF16)
    return hi, lo


def mm(a, b):
    return lax.dot_general(a, b, (((1,), (0,)), ((), ())), preferred_element_type=F32)


def mm_nt(a, b):
    return lax.dot_general(a, b, (((1,), (1,)), ((), ())), preferred_element_type=F32)


def flip(x):
    i = lax.broadcasted_iota(jnp.int32, (LOW, LOW), 0)
    j = lax.broadcasted_iota(jnp.int32, (LOW, LOW), 1)
    anti = jnp.where(i + j == LOW - 1, 1.0, 0.0).astype(BF16)
    hi, lo = split(x)
    r = mm(jnp.concatenate([hi, lo], 0), anti)
    return r[: x.shape[0]] + r[x.shape[0] :]


def slopes(rows_ref, cols_ref):
    along_x = (rows_ref[...].astype(F32) - 255.5) * 0.5
    along_y = (cols_ref[...].astype(F32) - 127.5) * 0.5
    radius = jnp.sqrt(along_x * along_x + along_y * along_y + 1600.0)
    return along_x / radius, along_y / radius, 80.0 / (radius * 1024.0)


def sides(v):
    out = []
    for h in range(NY_EL // LOW):
        a = v[(2 * h - TURN_IN) % 16]
        b = v[(2 * h + 1 - TURN_IN) % 16]
        top = jnp.concatenate([a[:, :64], b[:, :64]], 1)
        low = jnp.concatenate([a[:, 64:], b[:, 64:]], 1)
        out.append(jnp.concatenate([top, low], 0))
    return out


def pack_kernel(theta_ref, out_ref, in_ref, held_ref, sems):
    fetch = pltpu.make_async_copy(theta_ref, in_ref, sems.at[0])
    fetch.start()
    fetch.wait()
    v = in_ref[...]
    v = jnp.concatenate([v[:16], v[16:]], 1)
    for z in range(out_ref.shape[0]):
        held_ref[z] = v
    store = pltpu.make_async_copy(held_ref, out_ref, sems.at[1])
    store.start()
    store.wait()


def table_kernel(prow_ref, pcol_ref, rows_ref, low_ref, high_ref, x_ref, scale_ref):
    sx, sy, scale = slopes(prow_ref, pcol_ref)
    scale_ref[...] = scale
    sx = sx * 0.5
    sy = sy * 0.5
    low_k = lax.broadcasted_iota(jnp.int32, (LOW, CW), 0).astype(F32) + 0.5
    high_k = (lax.broadcasted_iota(jnp.int32, (8, CW), 0) * (2 * LOW)).astype(F32) + LOW
    lattice_x = rows_ref[...].astype(F32) - (NX_EL - 1) / 2.0
    for r in range(CHUNKS):
        cols = slice(CW * r, CW * r + CW)
        c, s = cos_sin_turns(low_k * sy[r : r + 1])
        hi, lo = split(c)
        low_ref[0:LOW, cols] = hi
        low_ref[2 * LOW : 3 * LOW, cols] = lo
        hi, lo = split(s)
        low_ref[LOW : 2 * LOW, cols] = hi
        low_ref[3 * LOW : 4 * LOW, cols] = lo
        c, s = cos_sin_turns(high_k * sy[r : r + 1])
        high_ref[0:4, cols] = c[0:4]
        high_ref[4:8, cols] = s[0:4]
        c, s = cos_sin_turns(lattice_x * sx[r : r + 1])
        x_ref[0:32, cols] = c
        x_ref[32:64, cols] = s


def field_kernel(theta_ref, low_ref, high_ref, x_ref, part_ref, u_ref):
    c, s = cos_sin_turns(theta_ref[...] * (1.0 / TWO_PI))
    re = sides(c)
    im = sides(s)
    back = flip(jnp.concatenate([re[0], im[0], re[2], im[2], re[4], im[4], re[6], im[6]], 0))
    even_re, even_im, odd_re, odd_im = [], [], [], []
    for h in range(4):
        m_re = back[64 * h : 64 * h + 32]
        m_im = back[64 * h + 32 : 64 * h + 64]
        p_re = re[2 * h + 1]
        p_im = im[2 * h + 1]
        cols = slice(LOW * 2 * h, LOW * 2 * h + LOW)
        u_ref[0:32, cols] = m_re
        u_ref[32:64, cols] = m_im
        cols = slice(LOW * (2 * h + 1), LOW * (2 * h + 2))
        u_ref[0:32, cols] = p_re
        u_ref[32:64, cols] = p_im
        even_re.append(p_re + m_re)
        even_im.append(p_im + m_im)
        odd_re.append(p_re - m_re)
        odd_im.append(p_im - m_im)
    rows = []
    for g in range(2):
        for sign in (1.0, -1.0):
            e_re, e_im, o_re, o_im = (v[2 + g] + sign * v[1 - g] for v in (even_re, even_im, odd_re, odd_im))
            rows.append(jnp.concatenate([e_re, -o_im], 1))
            rows.append(jnp.concatenate([e_im, o_re], 1))
    hi, lo = split(jnp.concatenate(rows, 0))
    left = jnp.concatenate([hi, hi, lo], 1)
    for r in range(CHUNKS):
        cols = slice(CW * r, CW * r + CW)
        p = mm(left, jnp.concatenate([low_ref[:, cols], low_ref[0 : 2 * LOW, cols]], 0))
        f_re = jnp.zeros((32, CW), F32)
        f_im = jnp.zeros((32, CW), F32)
        for g in range(2):
            hc = high_ref[g : g + 1, cols]
            hs = high_ref[4 + g : 5 + g, cols]
            q = p[128 * g : 128 * g + 128]
            f_re = f_re + (hc * q[0:32] - hs * q[96:128])
            f_im = f_im + (hc * q[32:64] + hs * q[64:96])
        xc = x_ref[0:32, cols]
        xs = x_ref[32:64, cols]
        part_ref[r : r + 1] = jnp.sum(xc * f_re - xs * f_im, 0, keepdims=True)
        part_ref[r + 4 : r + 5] = jnp.sum(xc * f_im + xs * f_re, 0, keepdims=True)


def gradient_kernel(
    parts_ref, direct_ref, noise_ref, scale_ref, low_ref, high_ref, x_ref, u_ref, field_ref, out_ref, w_ref
):
    scale = scale_ref[...]
    total = jnp.sum(parts_ref[...], 0)
    re = direct_ref[0:4] + scale * total[0:4]
    im = direct_ref[4:8] + scale * total[4:8]
    field_ref[0:4] = re
    field_ref[4:8] = im
    power = noise_ref[...] + re * re + im * im
    q_re = re * scale / power
    q_im = -im * scale / power
    for r in range(CHUNKS):
        cols = slice(CW * r, CW * r + CW)
        a = q_re[r : r + 1]
        b = q_im[r : r + 1]
        xc = x_ref[0:32, cols]
        xs = x_ref[32:64, cols]
        w_re = a * xc - b * xs
        w_im = a * xs + b * xc
        w = jnp.concatenate([w_re, w_im], 0)
        for g in range(2):
            hi, lo = split(w * high_ref[g : g + 1, cols])
            w_ref[128 * g : 128 * g + 64, cols] = hi
            w_ref[256 + 128 * g : 320 + 128 * g, cols] = lo
            hi, lo = split(w * high_ref[4 + g : 5 + g, cols])
            w_ref[128 * g + 64 : 128 * g + 128, cols] = hi
            w_ref[320 + 128 * g : 384 + 128 * g, cols] = lo
    first = mm_nt(w_ref[...], low_ref[0 : 2 * LOW])
    sums = first[:256] + first[256:] + mm_nt(w_ref[0:256], low_ref[2 * LOW :])
    blocks = [None] * 8
    for g in range(2):
        v = sums[128 * g : 128 * g + 128]
        cc = v[0:64, :LOW]
        cs = v[0:64, LOW:]
        sc = v[64:128, :LOW]
        ss = v[64:128, LOW:]
        minus = cc - ss
        plus = cc + ss
        added = cs + sc
        taken = cs - sc
        for n, real, imag in (
            (5 + 2 * g, minus, added),
            (4 + 2 * g, plus, -taken),
            (3 - 2 * g, plus, taken),
            (2 - 2 * g, minus, -added),
        ):
            s_re = real[:32] - imag[32:]
            s_im = real[32:] + imag[:32]
            cols = slice(LOW * n, LOW * n + LOW)
            blocks[n] = -2.0 * (u_ref[0:32, cols] * s_im + u_ref[32:64, cols] * s_re)
    back = flip(jnp.concatenate(blocks[0::2], 0))
    for n in range(8):
        d = blocks[n] if n % 2 else back[16 * n : 16 * n + 32]
        out_ref[(2 * n - TURN_OUT) % 16] = jnp.concatenate([d[:16, :64], d[16:, :64]], 1)
        out_ref[(2 * n + 1 - TURN_OUT) % 16] = jnp.concatenate([d[:16, 64:], d[16:, 64:]], 1)


def last_kernel(got_ref, held_ref, grad_ref, field_ref):
    total = jnp.sum(got_ref[...], 0)
    grad_ref[0:16] = total[:, :64]
    grad_ref[16:32] = total[:, 64:]
    for r in range(CHUNKS):
        cols = slice(CW * r, CW * r + CW)
        field_ref[0:1, cols] = held_ref[r : r + 1]
        field_ref[1:2, cols] = held_ref[r + 4 : r + 5]


def shards(theta, panel_rows, point_rows, point_cols, direct, noise):
    points = point_rows.shape[0]
    peers = lax.axis_size("pts")
    elems = lax.axis_size("elem")
    params = pltpu.CompilerParams(vmem_limit_bytes=40 << 20)
    packed = pltpu.CompilerParams(vmem_limit_bytes=40 << 20)
    sent = pl.pallas_call(
        pack_kernel,
        out_shape=jax.ShapeDtypeStruct((peers, 16, 128), F32),
        in_specs=[pl.BlockSpec(memory_space=pltpu.HBM)],
        out_specs=pl.BlockSpec(memory_space=pltpu.HBM),
        scratch_shapes=[
            pltpu.VMEM(theta.shape, F32),
            pltpu.VMEM((peers, 16, 128), F32),
            pltpu.SemaphoreType.DMA((2,)),
        ],
        compiler_params=params,
        name="pack",
    )(theta)
    along_in = [[(i + TURN_IN) % peers for i in range(peers)]]
    along_out = [[(i + TURN_OUT) % peers for i in range(peers)]]
    plane = [[(2 * i + 20) % elems + core for i in range(elems // 2)] for core in (0, 1)]
    angles = lax.all_to_all(sent, "pts", 0, 0, axis_index_groups=along_in, tiled=True)
    prow = point_rows.reshape(CHUNKS, CW)
    pcol = point_cols.reshape(CHUNKS, CW)
    direct = direct.reshape(8, CW)
    noise = noise.reshape(CHUNKS, CW)
    low, high, beam, scale = pl.pallas_call(
        table_kernel,
        out_shape=(
            jax.ShapeDtypeStruct((4 * LOW, points), BF16),
            jax.ShapeDtypeStruct((8, points), F32),
            jax.ShapeDtypeStruct((64, points), F32),
            jax.ShapeDtypeStruct((CHUNKS, CW), F32),
        ),
        compiler_params=params,
        name="tables",
    )(prow, pcol, panel_rows.reshape(32, 1))
    part, phasors = pl.pallas_call(
        field_kernel,
        out_shape=(
            jax.ShapeDtypeStruct((8, CW), F32),
            jax.ShapeDtypeStruct((64, NY_EL), F32),
        ),
        compiler_params=params,
        name="field",
    )(angles, low, high, beam)
    part, direct, noise = lax.optimization_barrier((part, direct, noise))
    part = part + lax.ppermute(part, "elem", [(i, i ^ 1) for i in range(elems)])
    parts = lax.all_to_all(jnp.broadcast_to(part[None], (elems // 2, 8, CW)), "elem", 0, 0, axis_index_groups=plane, tiled=True)
    field, grads = pl.pallas_call(
        gradient_kernel,
        out_shape=(
            jax.ShapeDtypeStruct((8, CW), F32),
            jax.ShapeDtypeStruct((peers, 16, 128), F32),
        ),
        scratch_shapes=[pltpu.VMEM((512, points), BF16)],
        compiler_params=packed,
        name="gradient",
    )(parts, direct, noise, scale, low, high, beam, phasors)
    got = lax.all_to_all(grads, "pts", 0, 0, axis_index_groups=along_out, tiled=True)
    return pl.pallas_call(
        last_kernel,
        out_shape=(
            jax.ShapeDtypeStruct(theta.shape, F32),
            jax.ShapeDtypeStruct((2, points), F32),
        ),
        compiler_params=params,
        name="last",
    )(got, field)


def solution(mesh):
    in_specs = (P("elem", "pts"), P("elem"), P("pts"), P("pts"), P(None, "pts"), P("pts"))
    out_specs = (P("elem", "pts"), P(None, "pts"))
    return jax.shard_map(shards, mesh=mesh, in_specs=in_specs, out_specs=out_specs, check_vma=False)
```
